256 devices in a mesh: leaf: 128 (over x, z, y), front: 2 (over core).
Axes of the slice: x: 4, y: 4, z: 8, core: 2. Of those that a mesh axis runs over, the one named last changes fastest.
Arguments:
- child_fronts: float32 [384, 2, 512, 1024], P('leaf', None, 'front'), may hold values from 0 to 16, as said below
- child_live: int32 [128], P('leaf'), may hold values from 1 to 3, as said below
- row_map: int32 [384, 4], P('leaf'), may hold values from 0 to 7, as said below
- parent_fronts: float32 [128, 2, 256, 1024], P('leaf', None, 'front'), may hold values from 0 to 16, as said below
Outputs:
- child_panels: float32 [384, 2, 512, 512], P('leaf', None, 'front')
- parent_panels: float32 [128, 2, 256, 512], P('leaf', None, 'front')
- parent_updates: float32 [128, 256, 512], P('leaf', 'front')
The draws below stay inside these ranges and needn't reach their ends.
Inputs may be any that keep to these rules, and one draw needn't show every extreme that they name: `child_fronts`: each front and each separator front is symmetric, and it and every separator front after the extend-add are positive definite. `parent_fronts`: symmetric as the child fronts. `child_live`: the two subtrees of leaf indices 2 * k and 2 * k + 1 hold at most 4 live fronts together; in every draw some subtree holds 3. `row_map`: each row names 4 different blocks of the separator, in increasing order.
All inputs are finite; a program needn't handle non-finite values.
Results may differ from the reference program's by a relative error of at most 0.000053.
Values sent between devices are 32-bit elements; how exact they have to be, the bound alone decides.
No kernel may reach another device: no remote copies, remote signals or barrier semaphores. Data moves between devices by JAX's collectives and lax.ppermute only.
A program may use at most 128 MiB of HBM per device.

```python
import jax
import jax.numpy as jnp
from jax import lax

FC = 1024
PIV = 512
FP = 1024
PPIV = 512
BLK = 128
CBLK = 4
SLOTS = 3
N_LEAF = 128


def symmetric_fronts(key, number, extent):
    front_keys = jax.random.split(key, number)

    def one_front(front_key):
        key_points, key_diagonal = jax.random.split(front_key, 2)
        points = jax.random.uniform(key_points, (extent, 3), jnp.float32, 0.0, 1.0)
        squares = jnp.sum(points * points, axis=1)
        inner = jnp.dot(points, points.T, precision=lax.Precision.HIGHEST)
        distance = jnp.sqrt(jnp.maximum(squares[:, None] + squares[None, :] - 2.0 * inner, 0.0))
        reach = 0.5 * extent ** (-1.0 / 3.0)
        kernel = jnp.exp(-distance / reach)
        kernel = 0.5 * (kernel + kernel.T)
        identity = jnp.eye(extent, dtype=jnp.float32)
        diagonal = jax.random.uniform(key_diagonal, (extent,), jnp.float32, 0.5, 1.5)
        matrix = kernel * (1.0 - identity) + (1.0 + diagonal)[:, None] * identity
        return matrix
    return lax.map(one_front, front_keys)


def draw_child_fronts(key, part):
    matrix = symmetric_fronts(jax.random.fold_in(key, 3), N_LEAF * SLOTS, FC)
    return matrix.reshape(N_LEAF * SLOTS, 2, FC // 2, FC)


def draw_parent_fronts(key, part):
    matrix = symmetric_fronts(jax.random.fold_in(key, 7), N_LEAF // 2, FP)
    matrix = matrix.reshape(N_LEAF // 2, 2, 2, FP // 4, FP).transpose(0, 2, 1, 3, 4)
    return matrix.reshape(N_LEAF, 2, FP // 4, FP)


def draw_child_live(key, part):
    pair_count = N_LEAF // 2
    key_heavy, key_other, key_flip, key_force = jax.random.split(jax.random.fold_in(key, 11), 4)
    heavy = jax.random.randint(key_heavy, (pair_count,), 0, 4) == 0
    forced = jax.random.randint(key_force, (), 0, pair_count)
    heavy = heavy | (jnp.arange(pair_count) == forced)
    partner = jax.random.randint(key_other, (pair_count,), 1, 3)
    first_chip = jnp.where(heavy, SLOTS, 1)
    second_chip = jnp.where(heavy, 1, partner)
    flipped = jax.random.randint(key_flip, (pair_count,), 0, 2) == 1
    even_chip = jnp.where(flipped, second_chip, first_chip)
    odd_chip = jnp.where(flipped, first_chip, second_chip)
    return jnp.stack([even_chip, odd_chip], axis=1).reshape(N_LEAF).astype(jnp.int32)


def draw_row_map(key, part):
    number = N_LEAF * SLOTS
    blocks = FP // BLK
    scores = jax.random.randint(jax.random.fold_in(key, 13), (number, blocks), 0, 1 << 20) * blocks + jnp.arange(blocks, dtype=jnp.int32)[None, :]
    chosen = jnp.argsort(scores, axis=1)[:, :FC // 2 // BLK]
    return jnp.sort(chosen, axis=1).astype(jnp.int32)


def setup_inputs(seed: int = 0) -> dict:
    seeds = jax.random.split(jax.random.key(seed), 5)
    child_fronts = draw_child_fronts(jax.random.fold_in(seeds[4], 71), 0)
    child_live = draw_child_live(jax.random.fold_in(seeds[4], 71), 0)
    row_map = draw_row_map(jax.random.fold_in(seeds[4], 71), 0)
    parent_fronts = draw_parent_fronts(jax.random.fold_in(seeds[4], 71), 0)
    return {"child_fronts": child_fronts, "child_live": child_live, "row_map": row_map, "parent_fronts": parent_fronts}


highest = lax.Precision.HIGHEST

def partial_factor(matrix, pivots):
    factor = jnp.linalg.cholesky(matrix[:pivots, :pivots])
    lower_panel = jax.scipy.linalg.solve_triangular(factor, matrix[pivots:, :pivots].T, lower=True).T
    update = matrix[pivots:, pivots:] - jnp.dot(lower_panel.astype(jnp.float32), lower_panel.T.astype(jnp.float32), precision=highest, preferred_element_type=jnp.float32)
    return (jnp.concatenate([factor, lower_panel], axis=0), update)

def reference(child_fronts, child_live, row_map, parent_fronts):
    total_fronts = N_LEAF * SLOTS
    fronts = child_fronts.reshape(total_fronts, FC, FC)
    slot_ids = jnp.arange(total_fronts, dtype=jnp.int32) % SLOTS
    active = slot_ids < jnp.repeat(child_live, SLOTS)

    def one_child(operands):
        matrix, is_live = operands
        panel_rows, update = partial_factor(matrix, PIV)
        return (jnp.where(is_live, panel_rows, 0.0), jnp.where(is_live, update, 0.0))
    panels, updates = lax.map(one_child, (fronts, active))
    child_panels = panels.reshape(total_fronts, 2, PIV, PIV)
    pair_count = N_LEAF // 2
    parent_blocks = FP // BLK
    parents = parent_fronts.reshape(pair_count, 2, 2, FP // 4, FP).transpose(0, 2, 1, 3, 4).reshape(pair_count, FP, FP)
    block_hot = (row_map[:, :, None] == jnp.arange(parent_blocks, dtype=jnp.int32)[None, None, :]).astype(jnp.float32)
    hot_pairs = block_hot.reshape(pair_count, 2 * SLOTS, CBLK, parent_blocks)
    tile_view = updates.reshape(pair_count, 2 * SLOTS, CBLK, BLK, CBLK, BLK)

    def one_parent(operands):
        parent, tile_block, hot_block = operands
        spread = jnp.einsum('karbs,kbp->karps', tile_block, hot_block, precision=highest)
        assembled = jnp.einsum('karps,kaq->qrps', spread, hot_block, precision=highest).reshape(FP, FP)
        return partial_factor(parent + assembled, PPIV)
    parent_panels_all, parent_updates_all = lax.map(one_parent, (parents, tile_view, hot_pairs))
    parent_panels = parent_panels_all.reshape(pair_count, 2, 2, FP // 4, PPIV).transpose(0, 2, 1, 3, 4).reshape(N_LEAF, 2, FP // 4, PPIV)
    parent_updates = parent_updates_all.reshape(N_LEAF, FP // 4, FP - PPIV)
    return (child_panels, parent_panels, parent_updates)
```

```python
import jax
import jax.numpy as jnp
from jax import lax
from jax.experimental import pallas as pl
from jax.experimental.pallas import tpu as pltpu
from jax.sharding import PartitionSpec as P

highest = lax.Precision.HIGHEST
TILE = 128
GROUP = 8
PAIRS = [(a, b) for a in range(4) for b in range(a + 1)]
f32 = jnp.float32


def times_transposed(first, second):
    return lax.dot_general(
        first, second, (((1,), (1,)), ((), ())), precision=highest, preferred_element_type=f32
    )


def spread(value):
    return jnp.broadcast_to(value, (GROUP, TILE))


def eliminate_tile(work, upper_ref, inverse_ref):
    row_id = lax.broadcasted_iota(jnp.int32, (TILE, TILE), 0)
    col_id = lax.broadcasted_iota(jnp.int32, (TILE, TILE), 1)
    work[:, TILE:] = jnp.where(row_id == col_id, 1.0, 0.0)
    sub = lax.broadcasted_iota(jnp.int32, (GROUP, TILE), 0)
    lane = lax.broadcasted_iota(jnp.int32, (GROUP, TILE), 1)
    groups = TILE // GROUP
    rows, ident = work[0:GROUP, :TILE], work[0:GROUP, TILE:]
    for g in range(groups):
        base = GROUP * g
        more = g + 1 < groups
        cols = [spread(rows[:, base + m : base + m + 1]) for m in range(GROUP)]
        if more:
            rows2 = work[base + GROUP : base + 2 * GROUP, :TILE]
            ident2 = work[base + GROUP : base + 2 * GROUP, TILE:]
            cols2 = [spread(rows2[:, base + m : base + m + 1]) for m in range(GROUP)]
        pivots = []
        for m in range(0, GROUP, 2):
            p = spread(cols[m][m : m + 1])
            q = spread(cols[m][m + 1 : m + 2])
            r = spread(cols[m + 1][m + 1 : m + 2])
            det = p * r - q * q
            inv_p = 1.0 / p
            inv_s = p * (1.0 / det)
            ratio = q * inv_p
            pivots += [p, det * inv_p]
            k1 = jnp.where(sub > m, cols[m] * inv_p, 0.0)
            k2 = jnp.where(sub > m + 1, (cols[m + 1] - cols[m] * ratio) * inv_s, 0.0)
            r1 = spread(rows[m : m + 1])
            r2 = spread(rows[m + 1 : m + 2]) - ratio * r1
            e1 = spread(ident[m : m + 1])
            e2 = spread(ident[m + 1 : m + 2]) - ratio * e1
            rows = rows - k1 * r1 - k2 * r2
            ident = ident - k1 * e1 - k2 * e2
            if more:
                n1 = cols2[m] * inv_p
                n2 = (cols2[m + 1] - cols2[m] * ratio) * inv_s
                rows2 = rows2 - n1 * r1 - n2 * r2
                ident2 = ident2 - n1 * e1 - n2 * e2
            for n in range(m + 2, GROUP):
                t1 = spread(cols[n][m : m + 1])
                t2 = spread(cols[n][m + 1 : m + 2]) - ratio * t1
                cols[n] = cols[n] - k1 * t1 - k2 * t2
                if more:
                    cols2[n] = cols2[n] - n1 * t1 - n2 * t2
        pivot = pivots[0]
        for m in range(1, GROUP):
            pivot = jnp.where(sub == m, pivots[m], pivot)
        scale = lax.rsqrt(pivot)
        upper = jnp.where(lane >= sub + base, rows * scale, 0.0)
        inverse = ident * scale
        upper_ref[base : base + GROUP, :] = upper
        inverse_ref[base : base + GROUP, :] = inverse
        if g + 2 < groups:
            low = base + 2 * GROUP
            change = lax.dot_general(
                upper,
                jnp.concatenate([upper, inverse], axis=1),
                (((0,), (0,)), ((), ())),
                precision=highest,
                preferred_element_type=f32,
            )
            work[low:, :] = work[low:, :] - change[low:, :]
        if more:
            rows, ident = rows2, ident2


def factor_columns(panel, work, upper_ref, inverse_of):
    tiles = panel.shape[0] // TILE
    for j in range(4):
        lo, hi = j * TILE, (j + 1) * TILE
        inverse_ref = inverse_of(j)
        work[:, :TILE] = panel[lo:hi, lo:hi]
        eliminate_tile(work, upper_ref, inverse_ref)
        panel[lo:hi, lo:hi] = upper_ref[...].T
        if j:
            panel[0:lo, lo:hi] = jnp.zeros((lo, TILE), f32)
        if j + 1 < tiles:
            panel[hi:, lo:hi] = times_transposed(panel[hi:, lo:hi], inverse_ref[...])
        for c in range(j + 1, 4):
            cl, ch = c * TILE, (c + 1) * TILE
            panel[cl:, cl:ch] = panel[cl:, cl:ch] - times_transposed(
                panel[cl:, lo:hi], panel[cl:ch, lo:hi]
            )


def fetch(cases, top, bottom, sems):
    for flag, first, second in cases:

        @pl.when(flag)
        def _(first=first, second=second):
            pltpu.make_async_copy(first, top, sems.at[0]).start()
            pltpu.make_async_copy(second, bottom, sems.at[1]).start()

    pltpu.make_async_copy(cases[0][1], top, sems.at[0]).wait()
    pltpu.make_async_copy(cases[0][2], bottom, sems.at[1]).wait()


def pivot_kernel(where_ref, other_ref, own, peer, guest0, guest1, out, inverses, work, upper, sems):
    core = where_ref[0]
    guest = jnp.logical_and(core == 1, other_ref[0] == 3)
    half = own.shape[2]
    cases = (
        (
            core == 0,
            own.at[0, 0, :, pl.ds(0, half)],
            peer.at[:, :],
        ),
        (
            jnp.logical_and(core == 1, jnp.logical_not(guest)),
            peer.at[:, pl.ds(0, half)],
            own.at[1, 0, :, pl.ds(0, 2 * half)],
        ),
        (guest, guest0.at[:, :], guest1.at[:, :]),
    )
    fetch(cases, out.at[pl.ds(0, half), pl.ds(0, half)], out.at[pl.ds(half, half), :], sems)
    factor_columns(out, work, upper, lambda j: inverses.at[j])


def lower_kernel(
    where_ref, other_ref, own, peer, guest0, guest1, factor, inverses, out, update, rows, sems
):
    core = where_ref[0]
    guest = jnp.logical_and(core == 1, other_ref[0] == 3)
    half = own.shape[2]
    part = 3 * half
    cases = (
        (core == 0, own.at[0, 1, :, pl.ds(0, part)], peer.at[:, :]),
        (
            jnp.logical_and(core == 1, jnp.logical_not(guest)),
            peer.at[:, pl.ds(0, part)],
            own.at[1, 1, :, :],
        ),
        (guest, guest0.at[:, :], guest1.at[:, :]),
    )
    fetch(cases, rows.at[pl.ds(0, half), pl.ds(0, part)], rows.at[pl.ds(half, half), :], sems)
    for j in range(4):
        lo, hi = j * TILE, (j + 1) * TILE
        rows[:, lo:hi] = times_transposed(rows[:, lo:hi], inverses[j])
        if j < 3:
            rows[:, hi : 4 * TILE] = rows[:, hi : 4 * TILE] - times_transposed(
                rows[:, lo:hi], factor[hi:, lo:hi]
            )
    for k, (a, b) in enumerate(PAIRS):
        update[k] = rows[
            a * TILE : (a + 1) * TILE, (4 + b) * TILE : (5 + b) * TILE
        ] - times_transposed(
            rows[a * TILE : (a + 1) * TILE, : 4 * TILE], rows[b * TILE : (b + 1) * TILE, : 4 * TILE]
        )
    for h in range(2):
        out[h, 0] = factor[h * half : (h + 1) * half, :]
        out[h, 1] = rows[h * half : (h + 1) * half, : 4 * TILE]


def parent_kernel(
    where_ref,
    own_ref,
    other_ref,
    front_own,
    front_peer,
    front_far,
    front_far_peer,
    u_own,
    u_peer,
    u_far,
    u_far_peer,
    panels,
    update,
    panel,
    row,
    work,
    upper,
    inverse,
):
    core, chip = where_ref[0], where_ref[1]
    width = 4 * TILE

    def tile_at(index):
        return pl.ds(pl.multiple_of(index * TILE, TILE), TILE)

    for source, c, g in (
        (front_own, chip, core),
        (front_peer, chip, 1 - core),
        (front_far, 1 - chip, core),
        (front_far_peer, 1 - chip, 1 - core),
    ):
        for t in range(2):
            panel[tile_at(4 * t + 2 * c + g), :] = source[t, :, :width]
    row[...] = front_own[1, :, width:]
    mine = 4 + 2 * chip + core
    for source, here, there, g in (
        (u_own, own_ref, other_ref, core),
        (u_peer, own_ref, other_ref, 1 - core),
        (u_far, other_ref, own_ref, core),
        (u_far_peer, other_ref, own_ref, 1 - core),
    ):
        guest = there[0] == 3
        live = jnp.logical_or(g == 0, jnp.logical_or(guest, here[0] >= 2))
        spots = [
            jnp.where(g == 0, here[1 + a], jnp.where(guest, there[9 + a], here[5 + a]))
            for a in range(4)
        ]
        for k, (a, b) in enumerate(PAIRS):
            ra, rb = spots[a], spots[b]

            @pl.when(jnp.logical_and(live, rb < 4))
            def _(k=k, ra=ra, rb=rb, source=source):
                spot = (tile_at(ra), tile_at(rb))
                panel[spot] = panel[spot] + source[k]

            @pl.when(jnp.logical_and(live, jnp.logical_and(rb >= 4, ra == mine)))
            def _(k=k, rb=rb, source=source):
                spot = (slice(None), tile_at(rb - 4))
                row[spot] = row[spot] + source[k]

            if a != b:

                @pl.when(jnp.logical_and(live, rb == mine))
                def _(k=k, ra=ra, source=source):
                    spot = (slice(None), tile_at(ra - 4))
                    row[spot] = row[spot] + source[k].T

    factor_columns(panel, work, upper, lambda j: inverse)
    panels[0] = panel[tile_at(mine - 4), :]
    panels[1] = panel[tile_at(mine), :]
    update[...] = row[...] - times_transposed(panel[tile_at(mine), :], panel[width:, :])


SMEM = pl.BlockSpec(memory_space=pltpu.SMEM)
VMEM = pl.BlockSpec(memory_space=pltpu.VMEM)
ANY = pl.BlockSpec(memory_space=pl.ANY)
TILE_SCRATCH = [pltpu.VMEM((TILE, 2 * TILE), f32), pltpu.VMEM((TILE, TILE), f32)]


def run(kernel, name, flops, shapes, specs, scratch, *operands):
    return pl.pallas_call(
        kernel,
        out_shape=[jax.ShapeDtypeStruct(s, f32) for s in shapes],
        in_specs=specs,
        out_specs=[VMEM] * len(shapes),
        scratch_shapes=scratch,
        name=name,
        cost_estimate=pl.CostEstimate(flops=flops, bytes_accessed=1 << 22, transcendentals=0),
        compiler_params=pltpu.CompilerParams(vmem_limit_bytes=40 << 20),
    )(*operands)


def on_device(child_fronts, child_live, row_map, parent_fronts):
    quarter = child_fronts.shape[2]
    pivots = 2 * quarter
    core = lax.axis_index("front")
    chip = lax.axis_index("leaf") % 2
    leaves = lax.axis_size("leaf")
    both = ("leaf", "front")

    def swap_core(value):
        return lax.ppermute(value, "front", [(0, 1), (1, 0)])

    def swap_chip(value):
        return lax.ppermute(value, "leaf", [(i, i ^ 1) for i in range(leaves)])

    def to_far(value, source, target):
        return lax.ppermute(
            value, both, [(2 * i + source, 2 * (i ^ 1) + target) for i in range(leaves)]
        )

    place = jnp.stack([core, chip]).astype(jnp.int32)
    facts = jnp.concatenate([child_live, row_map.reshape(-1)])
    other = swap_chip(facts)
    lent = lax.dynamic_index_in_dim(child_fronts, 1 - core, 0, keepdims=False)
    peer_top = swap_core(lent[0, :, :pivots])
    guest_top0 = to_far(child_fronts[2, 0, :, :quarter], 0, 1)
    guest_top1 = to_far(child_fronts[2, 0, :, :pivots], 1, 1)
    peer_low = swap_core(lent[1])
    guest_low0 = to_far(child_fronts[2, 1, :, : 3 * quarter], 0, 1)
    guest_low1 = to_far(child_fronts[2, 1], 1, 1)
    front_own = parent_fronts[0]
    front_part = front_own[:, :, :pivots]
    front_peer = swap_core(front_part)
    front_far = swap_chip(front_part)
    front_far_peer = swap_core(front_far)

    factor, inverses = run(
        pivot_kernel,
        "pivot",
        10**10,
        [(pivots, pivots), (4, TILE, TILE)],
        [SMEM, SMEM, ANY, ANY, ANY, ANY],
        TILE_SCRATCH + [pltpu.SemaphoreType.DMA((2,))],
        place,
        other,
        child_fronts,
        peer_top,
        guest_top0,
        guest_top1,
    )
    halves, update = run(
        lower_kernel,
        "lower",
        2 * 10**9,
        [(2, 2, quarter, pivots), (len(PAIRS), TILE, TILE)],
        [SMEM, SMEM, ANY, ANY, ANY, ANY, VMEM, VMEM],
        [pltpu.VMEM((pivots, 2 * pivots), f32), pltpu.SemaphoreType.DMA((2,))],
        place,
        other,
        child_fronts,
        peer_low,
        guest_low0,
        guest_low1,
        factor,
        inverses,
    )
    u_peer = swap_core(update)
    u_far = swap_chip(update)
    u_far_peer = swap_core(u_far)
    held = lax.dynamic_index_in_dim(halves, core, 0, keepdims=False)
    given = lax.dynamic_index_in_dim(halves, 1 - core, 0, keepdims=False)
    given, sent, u_far_peer = lax.optimization_barrier((given, halves, u_far_peer))
    taken = swap_core(given)
    back0 = to_far(sent[0], 1, 0)
    back1 = to_far(sent[1], 1, 1)
    panels, parent_update = run(
        parent_kernel,
        "parent",
        10**10,
        [(2, TILE, pivots), (TILE, pivots)],
        [SMEM] * 3 + [VMEM] * 8,
        [pltpu.VMEM((2 * pivots, pivots), f32), pltpu.VMEM((TILE, pivots), f32)]
        + TILE_SCRATCH
        + [pltpu.VMEM((TILE, TILE), f32)],
        place,
        facts,
        other,
        front_own,
        front_peer,
        front_far,
        front_far_peer,
        update,
        u_peer,
        u_far,
        u_far_peer,
    )
    live = child_live[0]
    first = jnp.where(core == 0, held, taken)
    second = jnp.where(live >= 2, jnp.where(core == 0, taken, held), 0.0)
    third = jnp.where(live == 3, jnp.where(core == 0, back0, back1), 0.0)
    child_panels = jnp.stack([first, second, third])
    return (child_panels, panels[None], parent_update[None])


def solution(mesh):
    placed = (
        P("leaf", None, "front", None),
        P("leaf"),
        P("leaf", None),
        P("leaf", None, "front", None),
    )
    return jax.shard_map(
        on_device,
        mesh=mesh,
        in_specs=placed,
        out_specs=(
            P("leaf", None, "front", None),
            P("leaf", None, "front", None),
            P("leaf", "front", None),
        ),
        check_vma=False,
    )
```

```python
import jax
import jax.numpy as jnp
from jax import lax
from jax.experimental import pallas as pl
from jax.experimental.pallas import tpu as pltpu
from jax.sharding import PartitionSpec as P

highest = lax.Precision.HIGHEST
TILE = 128
GROUP = 8
PAIRS = [(a, b) for a in range(4) for b in range(a + 1)]
HALF = len(PAIRS) // 2
f32 = jnp.float32


def times_transposed(first, second):
    return lax.dot_general(
        first, second, (((1,), (1,)), ((), ())), precision=highest, preferred_element_type=f32
    )


def spread(value):
    return jnp.broadcast_to(value, (GROUP, TILE))


def column(value, index):
    lanes = jnp.full((GROUP, TILE), index, jnp.int32)
    return jnp.take_along_axis(value, lanes, axis=1, mode="promise_in_bounds")


def eliminate(load, inverse_ref, carry):
    sub = lax.broadcasted_iota(jnp.int32, (GROUP, TILE), 0)
    lane = lax.broadcasted_iota(jnp.int32, (GROUP, TILE), 1)
    groups = TILE // GROUP
    tile = [load(i) for i in range(groups)]
    cols = [column(tile[0], m) for m in range(GROUP)]
    for g in range(groups):
        base = GROUP * g
        more = g + 1 < groups
        raw = [[column(tile[i], base + m) for m in range(GROUP)] for i in range(g + 1, groups)]
        inside = (lane >= base) & (lane < base + GROUP)
        rows = jnp.where(inside, jnp.where(lane - base == sub, 1.0, 0.0), tile[g])
        if more:
            below = list(raw[0])
            if carry:
                ahead = [column(tile[g + 1], base + GROUP + m) for m in range(GROUP)]
            else:
                next_rows = jnp.where(inside, 0.0, tile[g + 1])
        pivots = None
        for m in range(GROUP):
            pivot = spread(cols[m][m : m + 1])
            inv = 1.0 / pivot
            pivots = pivot if m == 0 else jnp.where(sub == m, pivot, pivots)
            factor = jnp.where(sub > m, cols[m] * inv, 0.0)
            row = spread(rows[m : m + 1])
            rows = rows - factor * row
            if more:
                factor2 = below[m] * inv
                if not carry:
                    next_rows = next_rows - factor2 * row
            for n in range(m + 1, GROUP):
                entry = spread(cols[n][m : m + 1])
                cols[n] = cols[n] - factor * entry
                if more:
                    below[n] = below[n] - factor2 * entry
            if more and carry:
                for n in range(GROUP):
                    ahead[n] = ahead[n] - factor2 * spread(below[m][n : n + 1])
        scale = lax.rsqrt(pivots)
        inverse_ref[base : base + GROUP, :] = jnp.where(lane < base + GROUP, rows, 0.0) * scale
        if more:
            inv = 1.0 / pivots
            solved = rows * inv
            for m in range(GROUP - 1, 0, -1):
                solved = solved - jnp.where(sub < m, cols[m] * inv, 0.0) * spread(
                    solved[m : m + 1]
                )
            spans = [spread(solved[m : m + 1]) for m in range(GROUP)]
            for i in range(g + 1 if carry else g + 2, groups):
                terms = [x * z for x, z in zip(raw[i - g - 1], spans)]
                while len(terms) > 1:
                    terms = [x + y for x, y in zip(terms[::2], terms[1::2])]
                tile[i] = jnp.where(inside, 0.0, tile[i]) - terms[0]
            if carry:
                cols = ahead
            else:
                tile[g + 1] = next_rows
                cols = [column(next_rows, base + GROUP + m) for m in range(GROUP)]
        yield


def factor_pivots(panels, inverses, carry):
    row_id = lax.broadcasted_iota(jnp.int32, (TILE, TILE), 0)
    col_id = lax.broadcasted_iota(jnp.int32, (TILE, TILE), 1)
    for j in range(4):
        lo, hi = j * TILE, (j + 1) * TILE
        running = [
            eliminate(
                lambda i, panel=panel: panel[lo + GROUP * i : lo + GROUP * (i + 1), lo:hi],
                inverse.at[j],
                carry,
            )
            for panel, inverse in zip(panels, inverses)
        ]
        for _ in zip(*running):
            pass
        if j < 3:
            ch = hi + TILE
            for panel, inverse in zip(panels, inverses):
                panel[hi:ch, lo:hi] = times_transposed(panel[hi:ch, lo:hi], inverse[j])
                panel[hi:ch, hi:ch] = panel[hi:ch, hi:ch] - times_transposed(
                    panel[hi:ch, lo:hi], panel[hi:ch, lo:hi]
                )
        for panel, inverse in zip(panels, inverses):
            if j < 2:
                ch = hi + TILE
                panel[ch:, lo:hi] = times_transposed(panel[ch:, lo:hi], inverse[j])
                panel[ch:, hi:ch] = panel[ch:, hi:ch] - times_transposed(
                    panel[ch:, lo:hi], panel[hi:ch, lo:hi]
                )
            for c in range(j + 2, 4):
                cl, ch = c * TILE, (c + 1) * TILE
                panel[cl:, cl:ch] = panel[cl:, cl:ch] - times_transposed(
                    panel[cl:, lo:hi], panel[cl:ch, lo:hi]
                )
            whole = times_transposed(panel[lo:hi, lo:hi], inverse[j])
            panel[lo:hi, lo:hi] = jnp.where(row_id >= col_id, whole, 0.0)
            if j:
                panel[0:lo, lo:hi] = jnp.zeros((lo, TILE), f32)


def split_left(value):
    high = value.astype(jnp.bfloat16)
    low = (value - high.astype(f32)).astype(jnp.bfloat16)
    return jnp.concatenate([high, low, high], axis=1)


def split_right(value):
    high = value.astype(jnp.bfloat16)
    low = (value - high.astype(f32)).astype(jnp.bfloat16)
    return jnp.concatenate([high, high, low], axis=1)


def parts_product(left, right):
    return lax.dot_general(left, right, (((1,), (1,)), ((), ())), preferred_element_type=f32)


def solve_rows(rows, factor, inverses):
    for j in range(4):
        lo, hi = j * TILE, (j + 1) * TILE
        rows[:, lo:hi] = parts_product(split_left(rows[:, lo:hi]), split_right(inverses[j]))
        if j < 3:
            rows[:, hi : 4 * TILE] = rows[:, hi : 4 * TILE] - parts_product(
                split_left(rows[:, lo:hi]), split_right(factor[hi:, lo:hi])
            )


def fetch_fronts(core, own, peer, t, first, columns, buffers, sems):
    half = own.shape[2]
    mine = pl.ds(pl.multiple_of(core * half, half), half)
    theirs = pl.ds(pl.multiple_of((1 - core) * half, half), half)
    span = pl.ds(first, columns)
    copies = []
    for k in range(2):
        sources = ((own.at[core + k, t, :, span], mine), (peer.at[k, :, span], theirs))
        pair = [
            pltpu.make_async_copy(source, buffers[k].at[spot, span], sems.at[2 * k + n])
            for n, (source, spot) in enumerate(sources)
        ]
        for copy in pair:
            copy.start()
        copies.append(pair)
    return copies


def wait_all(copies):
    for copy in copies:
        copy.wait()


def pivot_kernel(place, own, peer, factors, inverses, sems):
    panels = [factors.at[k] for k in range(2)]
    copies = fetch_fronts(place[0], own, peer, 0, 0, factors.shape[2], panels, sems)
    for pair in copies:
        wait_all(pair)
    factor_pivots(panels, [inverses.at[k] for k in range(2)], False)


def lower_kernel(
    place,
    live,
    maps,
    own,
    peer,
    factors,
    inverses,
    front,
    held,
    given,
    keep_pivot,
    give_pivot,
    keep_low,
    give_low,
    rows0,
    rows1,
    left,
    right,
    pivot_sum,
    low_sum,
    sems,
):
    core, chip = place[0], place[1]
    half = own.shape[2]
    pivots = factors.shape[2]
    buffers = [rows0, rows1]
    solved = fetch_fronts(core, own, peer, 1, 0, pivots, buffers, sems.at[0])
    others = fetch_fronts(core, own, peer, 1, pivots, pivots, buffers, sems.at[1])
    mine = pl.ds(pl.multiple_of(core * half, half), half)
    theirs = pl.ds(pl.multiple_of((1 - core) * half, half), half)
    stores = [
        pltpu.make_async_copy(factors.at[k, mine, :], held.at[k, 0], sems.at[2, k])
        for k in range(2)
    ]
    stores.append(pltpu.make_async_copy(factors.at[core, theirs, :], given.at[0], sems.at[2, 2]))
    for store in stores:
        store.start()
    pivot_sum[...] = jnp.zeros(pivot_sum.shape, f32)
    low_sum[...] = jnp.zeros(low_sum.shape, f32)
    place_row = 2 * chip + core
    for j in range(4):
        part = slice(j * TILE, (j + 1) * TILE)
        rest = slice((4 + j) * TILE, (5 + j) * TILE)

        @pl.when(j <= place_row)
        def _(j=j, part=part):
            pivot_sum[((place_row * (place_row + 1)) >> 1) + j] = front[0, :, part]

        low_sum[chip, 4 * core + j] = front[1, :, part]
        low_sum[core, 8 + 4 * chip + j] = front[1, :, rest]
    for k in range(2):
        rows = buffers[k]
        wait_all(solved[k])
        solve_rows(rows, factors.at[k], inverses.at[k])
        store = pltpu.make_async_copy(
            rows.at[mine, pl.ds(0, pivots)], held.at[k, 1], sems.at[3, k]
        )
        store.start()
        stores.append(store)
        store = pltpu.make_async_copy(
            rows.at[theirs, pl.ds(0, pivots)], given.at[1], sems.at[3, 2]
        )
        pl.when(core == k)(store.start)
        if k:
            stores.append(store)
        left[k] = split_left(rows[:, :pivots])
        right[k] = split_right(rows[:, :pivots])

    def contribute(k, slot, pairs):
        rows = buffers[k]
        for a, b in pairs:
            first = slice(a * TILE, (a + 1) * TILE)
            second = slice(b * TILE, (b + 1) * TILE)
            there = slice((4 + b) * TILE, (5 + b) * TILE)
            block = rows[first, there] - parts_product(left[k, first], right[k, second])
            ra, rb = maps[slot, a], maps[slot, b]

            @pl.when(ra < 4)
            def _():
                spot = ((ra * (ra + 1)) >> 1) + rb
                pivot_sum[spot] = pivot_sum[spot] + block

            @pl.when(jnp.logical_and(ra >= 4, rb < 4))
            def _():
                spot = (ra - 4) >> 1, (ra & 1) * 4 + rb
                low_sum[spot] = low_sum[spot] + block

            @pl.when(rb >= 4)
            def _():
                spot = ra & 1, 8 + ((ra - 4) >> 1) * 4 + rb - 4
                low_sum[spot] = low_sum[spot] + block
                if a != b:
                    spot = rb & 1, 8 + ((rb - 4) >> 1) * 4 + ra - 4
                    low_sum[spot] = low_sum[spot] + block.T

    for k in range(2):
        slot = core + k
        wait_all(others[k])
        pl.when(core == 0 if k == 0 else live[0] > slot)(
            lambda k=k, slot=slot: contribute(k, slot, PAIRS[:HALF])
        )
        pl.when(live[0] > slot if k == 0 else jnp.logical_and(core == 1, live[0] > slot))(
            lambda k=k, slot=slot: contribute(k, slot, PAIRS[HALF:])
        )
    keep_pivot[...] = pivot_sum[pl.ds(core * HALF, HALF)]
    give_pivot[...] = pivot_sum[pl.ds((1 - core) * HALF, HALF)]
    keep_low[...] = low_sum[core]
    give_low[...] = low_sum[1 - core]
    wait_all(stores)


def parent_pivot_kernel(
    place, live, own, other, held, taken, factor, inverses, children, stage, blank, sems
):
    core = place[0]
    loads = [pltpu.make_async_copy(held.at[k], stage.at[k], sems.at[k]) for k in range(2)]
    loads.append(pltpu.make_async_copy(taken, stage.at[2], sems.at[2]))
    for copy in loads:
        copy.start()
    blank[...] = jnp.zeros(blank.shape, f32)
    for side in range(2):

        @pl.when(core == side)
        def _(side=side):
            for n, (a, b) in enumerate(PAIRS):
                source = own if n // HALF == side else other
                factor[a * TILE : (a + 1) * TILE, b * TILE : (b + 1) * TILE] = source[n % HALF]

    for copy in loads:
        copy.wait()
    spots = [
        jnp.where(core == 0, 0, 2),
        jnp.where(core == 0, 1, 0),
        jnp.where(core == 0, 2, 1),
    ]
    stores = []
    for slot in range(3):
        store = pltpu.make_async_copy(stage.at[spots[slot]], children.at[slot], sems.at[slot])
        clear = pltpu.make_async_copy(blank, children.at[slot], sems.at[slot])

        @pl.when(live[0] > slot)
        def _(store=store):
            store.start()

        @pl.when(live[0] <= slot)
        def _(clear=clear):
            clear.start()

        stores.append(store)
    factor_pivots([factor], [inverses], True)
    for store in stores:
        store.wait()


def parent_lower_kernel(place, factor, inverses, own, other, corner, panels, update, rows):
    core, chip = place[0], place[1]
    for side in range(2):

        @pl.when(core == side)
        def _(side=side):
            for n in range(16):
                source = own if n // 8 == side else other
                rows[n // 4 * TILE : (n // 4 + 1) * TILE, n % 4 * TILE : (n % 4 + 1) * TILE] = (
                    source[n % 8]
                )

    solve_rows(rows, factor, inverses)
    mine = pl.ds(pl.multiple_of((2 * chip + core) * TILE, TILE), TILE)
    panels[0] = factor[mine, :]
    panels[1] = rows[mine, :]
    left = split_left(rows[mine, :])
    for j in range(4):
        part = slice(j * TILE, (j + 1) * TILE)
        update[:, part] = corner[j] - parts_product(left, split_right(rows[part, :]))


SMEM = pl.BlockSpec(memory_space=pltpu.SMEM)
VMEM = pl.BlockSpec(memory_space=pltpu.VMEM)
ANY = pl.BlockSpec(memory_space=pl.ANY)


def run(kernel, name, flops, shapes, specs, scratch, *operands, out_specs=None):
    return pl.pallas_call(
        kernel,
        out_shape=[jax.ShapeDtypeStruct(s, f32) for s in shapes],
        in_specs=specs,
        out_specs=out_specs or [VMEM] * len(shapes),
        scratch_shapes=scratch,
        name=name,
        cost_estimate=pl.CostEstimate(flops=flops, bytes_accessed=1 << 22, transcendentals=0),
        compiler_params=pltpu.CompilerParams(vmem_limit_bytes=48 << 20),
    )(*operands)


def on_device(child_fronts, child_live, row_map, parent_fronts):
    quarter = child_fronts.shape[2]
    pivots = 2 * quarter
    core = lax.axis_index("front")
    chip = lax.axis_index("leaf") % 2
    leaves = lax.axis_size("leaf")
    blocks = (TILE, TILE)

    def swap_core(value):
        return lax.ppermute(value, "front", [(0, 1), (1, 0)])

    def swap_chip(value):
        return lax.ppermute(value, "leaf", [(i, i ^ 1) for i in range(leaves)])

    place = jnp.stack([core, chip]).astype(jnp.int32)
    top = lax.dynamic_slice(child_fronts, (1 - core, 0, 0, 0), (2, 1, quarter, pivots))[:, 0]
    peer_top = swap_core(top)
    low = lax.dynamic_slice(child_fronts, (1 - core, 1, 0, 0), (2, 1, quarter, 2 * pivots))[:, 0]
    peer_low = swap_core(low)
    factors, inverses = run(
        pivot_kernel,
        "pivot",
        10**10,
        [(2, pivots, pivots), (2, 4, *blocks)],
        [SMEM, ANY, ANY],
        [pltpu.SemaphoreType.DMA((4,))],
        place,
        child_fronts,
        peer_top,
    )
    held, given, keep_pivot, give_pivot, keep_low, give_low = run(
        lower_kernel,
        "lower",
        4 * 10**9,
        [
            (2, 2, quarter, pivots),
            (2, quarter, pivots),
            (HALF, *blocks),
            (HALF, *blocks),
            (16, *blocks),
            (16, *blocks),
        ],
        [SMEM, SMEM, SMEM, ANY, ANY, VMEM, VMEM, VMEM],
        [
            pltpu.VMEM((pivots, 2 * pivots), f32),
            pltpu.VMEM((pivots, 2 * pivots), f32),
            pltpu.VMEM((2, pivots, 3 * pivots), jnp.bfloat16),
            pltpu.VMEM((2, pivots, 3 * pivots), jnp.bfloat16),
            pltpu.VMEM((2 * HALF, *blocks), f32),
            pltpu.VMEM((2, 16, *blocks), f32),
            pltpu.SemaphoreType.DMA((4, 4)),
        ],
        place,
        child_live,
        row_map,
        child_fronts,
        peer_low,
        factors,
        inverses,
        parent_fronts[0],
        out_specs=[ANY, ANY] + [VMEM] * 4,
    )
    chip_pivot = keep_pivot + swap_core(give_pivot)
    give_low, given, far_pivot = lax.optimization_barrier((give_low, given, chip_pivot))
    taken = swap_core(given)
    half_pivot = chip_pivot + swap_chip(far_pivot)
    chip_low = keep_low + swap_core(give_low)
    chip_rows = chip_low[8:].reshape(2, 4, *blocks)
    own_rows = lax.dynamic_index_in_dim(chip_rows, chip, 0, keepdims=False)
    far_rows = lax.dynamic_index_in_dim(chip_rows, 1 - chip, 0, keepdims=False)
    half_pivot, far_low, far_rows = lax.optimization_barrier(
        (half_pivot, chip_low[:8], far_rows)
    )
    other_pivot = swap_core(half_pivot)
    arrived_low = swap_chip(far_low)
    arrived_rows = swap_chip(far_rows)
    factor, parent_inverses, child_panels = run(
        parent_pivot_kernel,
        "parent_pivot",
        10**10,
        [(pivots, pivots), (4, *blocks), child_fronts.shape[:3] + (pivots,)],
        [SMEM, SMEM, VMEM, VMEM, ANY, ANY],
        [
            pltpu.VMEM((3, 2, quarter, pivots), f32),
            pltpu.VMEM((2, quarter, pivots), f32),
            pltpu.SemaphoreType.DMA((3,)),
        ],
        place,
        child_live,
        half_pivot,
        other_pivot,
        held,
        taken,
        out_specs=[VMEM, VMEM, ANY],
    )
    factor, arrived_low, arrived_rows = lax.optimization_barrier(
        (factor, arrived_low, arrived_rows)
    )
    half_low = chip_low[:8] + arrived_low
    corner = own_rows + arrived_rows
    other_low = swap_core(half_low)
    panels, update = run(
        parent_lower_kernel,
        "parent_lower",
        10**9,
        [(2, TILE, pivots), (TILE, pivots)],
        [SMEM] + [VMEM] * 5,
        [pltpu.VMEM((pivots, pivots), f32)],
        place,
        factor,
        parent_inverses,
        half_low,
        other_low,
        corner,
    )
    return (child_panels, panels[None], update[None])


def solution(mesh):
    placed = (
        P("leaf", None, "front", None),
        P("leaf"),
        P("leaf", None),
        P("leaf", None, "front", None),
    )
    return jax.shard_map(
        on_device,
        mesh=mesh,
        in_specs=placed,
        out_specs=(
            P("leaf", None, "front", None),
            P("leaf", None, "front", None),
            P("leaf", "front", None),
        ),
        check_vma=False,
    )
```

```python
import jax
import jax.numpy as jnp
from jax import lax
from jax.experimental import pallas as pl
from jax.experimental.pallas import tpu as pltpu
from jax.sharding import PartitionSpec as P

highest = lax.Precision.HIGHEST
TILE = 128
GROUP = 8
PAIRS = [(a, b) for a in range(4) for b in range(a + 1)]
HALF = len(PAIRS) // 2
f32 = jnp.float32


def times_transposed(first, second):
    return lax.dot_general(
        first, second, (((1,), (1,)), ((), ())), precision=highest, preferred_element_type=f32
    )


def spread(value):
    return jnp.broadcast_to(value, (GROUP, TILE))


def column(value, index):
    lanes = jnp.full((GROUP, TILE), index, jnp.int32)
    return jnp.take_along_axis(value, lanes, axis=1, mode="promise_in_bounds")


def eliminate(load, inverse_ref):
    sub = lax.broadcasted_iota(jnp.int32, (GROUP, TILE), 0)
    lane = lax.broadcasted_iota(jnp.int32, (GROUP, TILE), 1)
    groups = TILE // GROUP
    tile = [load(i) for i in range(groups)]
    yield
    cols = [column(tile[0], m) for m in range(GROUP)]
    for g in range(groups):
        base = GROUP * g
        more = g + 1 < groups
        raw = [[column(tile[i], base + m) for m in range(GROUP)] for i in range(g + 1, groups)]
        inside = (lane >= base) & (lane < base + GROUP)
        rows = jnp.where(inside, jnp.where(lane - base == sub, 1.0, 0.0), tile[g])
        if more:
            below = list(raw[0])
            ahead = [column(tile[g + 1], base + GROUP + m) for m in range(GROUP)]
        pivots = None
        for m in range(GROUP):
            pivot = spread(cols[m][m : m + 1])
            inv = 1.0 / pivot
            pivots = pivot if m == 0 else jnp.where(sub == m, pivot, pivots)
            factor = jnp.where(sub > m, cols[m] * inv, 0.0)
            rows = rows - factor * spread(rows[m : m + 1])
            if more:
                factor2 = below[m] * inv
            for n in range(m + 1, GROUP):
                entry = spread(cols[n][m : m + 1])
                cols[n] = cols[n] - factor * entry
                if more:
                    below[n] = below[n] - factor2 * entry
            if more:
                for n in range(GROUP):
                    ahead[n] = ahead[n] - factor2 * spread(below[m][n : n + 1])
        scale = lax.rsqrt(pivots)
        inverse_ref[base : base + GROUP, :] = jnp.where(lane < base + GROUP, rows, 0.0) * scale
        if more:
            inv = 1.0 / pivots
            solved = rows * inv
            for m in range(GROUP - 1, 0, -1):
                solved = solved - jnp.where(sub < m, cols[m] * inv, 0.0) * spread(
                    solved[m : m + 1]
                )
            spans = [spread(solved[m : m + 1]) for m in range(GROUP)]
            for i in range(g + 1, groups):
                terms = [x * z for x, z in zip(raw[i - g - 1], spans)]
                while len(terms) > 1:
                    terms = [x + y for x, y in zip(terms[::2], terms[1::2])]
                tile[i] = jnp.where(inside, 0.0, tile[i]) - terms[0]
            cols = ahead
        yield


GRID = 6


def factor_pivots(grids, inverses, beside=None):
    row_id = lax.broadcasted_iota(jnp.int32, (TILE, TILE), 0)
    col_id = lax.broadcasted_iota(jnp.int32, (TILE, TILE), 1)

    def step(j, carry):
        if beside is not None:
            pl.when(j == 1)(beside)
        before = jnp.where(j == 0, 2, j - 1)
        running = [
            eliminate(
                lambda i, grid=grid: grid[
                    j * (GRID + 1), GROUP * i : GROUP * (i + 1), :
                ],
                inverse.at[j],
            )
            for grid, inverse in zip(grids, inverses)
        ]
        for steps in running:
            next(steps)
        for grid, inverse in zip(grids, inverses):

            def spot(r, c):
                return (before + r) * GRID + before + c

            near = grid[spot(1, 0)]
            both = jnp.concatenate([grid[spot(2, 0)], grid[spot(3, 0)]])
            both = times_transposed(both, inverse[before])
            grid[spot(2, 0)] = both[:TILE]
            grid[spot(3, 0)] = both[TILE:]
            change = times_transposed(both, near)
            grid[spot(2, 1)] = grid[spot(2, 1)] - change[:TILE]
            grid[spot(3, 1)] = grid[spot(3, 1)] - change[TILE:]
            change = times_transposed(both, both[:TILE])
            grid[spot(2, 2)] = grid[spot(2, 2)] - change[:TILE]
            grid[spot(3, 2)] = grid[spot(3, 2)] - change[TILE:]
            grid[spot(3, 3)] = grid[spot(3, 3)] - times_transposed(both[TILE:], both[TILE:])
        for _ in zip(*running):
            pass
        for grid, inverse in zip(grids, inverses):
            below = (j + 1) * GRID + j
            solved = times_transposed(grid[below], inverse[j])
            grid[below] = solved
            grid[below + 1] = grid[below + 1] - times_transposed(solved, solved)
            whole = times_transposed(grid[j * (GRID + 1)], inverse[j])
            grid[j * (GRID + 1)] = jnp.where(row_id >= col_id, whole, 0.0)
        return carry

    lax.fori_loop(0, 4, step, 0)


def matrix_to_grid(matrix, grid):
    for a, b in PAIRS:
        grid[a * GRID + b] = matrix[a * TILE : (a + 1) * TILE, b * TILE : (b + 1) * TILE]


def grid_to_matrix(grid, matrix):
    for a in range(4):
        for b in range(4):
            part = grid[a * GRID + b] if b <= a else jnp.zeros((TILE, TILE), f32)
            matrix[a * TILE : (a + 1) * TILE, b * TILE : (b + 1) * TILE] = part


def split_left(value):
    high = value.astype(jnp.bfloat16)
    low = (value - high.astype(f32)).astype(jnp.bfloat16)
    return jnp.concatenate([high, low, high], axis=1)


def split_right(value):
    high = value.astype(jnp.bfloat16)
    low = (value - high.astype(f32)).astype(jnp.bfloat16)
    return jnp.concatenate([high, high, low], axis=1)


def parts_product(left, right):
    return lax.dot_general(left, right, (((1,), (1,)), ((), ())), preferred_element_type=f32)


def solve_rows(rows, factor, inverses):
    for j in range(4):
        lo, hi = j * TILE, (j + 1) * TILE
        rows[:, lo:hi] = parts_product(split_left(rows[:, lo:hi]), split_right(inverses[j]))
        if j < 3:
            rows[:, hi : 4 * TILE] = rows[:, hi : 4 * TILE] - parts_product(
                split_left(rows[:, lo:hi]), split_right(factor[hi:, lo:hi])
            )


def fetch_fronts(core, own, peer, t, first, columns, buffers, sems):
    half = own.shape[2]
    mine = pl.ds(pl.multiple_of(core * half, half), half)
    theirs = pl.ds(pl.multiple_of((1 - core) * half, half), half)
    span = pl.ds(first, columns)
    copies = []
    for k in range(2):
        sources = ((own.at[core + k, t, :, span], mine), (peer.at[k, :, span], theirs))
        pair = [
            pltpu.make_async_copy(source, buffers[k].at[spot, span], sems.at[2 * k + n])
            for n, (source, spot) in enumerate(sources)
        ]
        for copy in pair:
            copy.start()
        copies.append(pair)
    return copies


def wait_all(copies):
    for copy in copies:
        copy.wait()


def pivot_kernel(place, own, peer, factors, inverses, grid0, grid1, sems):
    panels = [factors.at[k] for k in range(2)]
    grids = [grid0, grid1]
    copies = fetch_fronts(place[0], own, peer, 0, 0, factors.shape[2], panels, sems)
    for pair, panel, grid in zip(copies, panels, grids):
        wait_all(pair)
        matrix_to_grid(panel, grid)
    factor_pivots(grids, [inverses.at[k] for k in range(2)])
    for panel, grid in zip(panels, grids):
        grid_to_matrix(grid, panel)


def lower_kernel(
    place,
    live,
    maps,
    own,
    peer,
    factors,
    inverses,
    front,
    held,
    given,
    keep_pivot,
    give_pivot,
    keep_low,
    give_low,
    rows0,
    rows1,
    left,
    right,
    pivot_sum,
    low_sum,
    sems,
):
    core, chip = place[0], place[1]
    half = own.shape[2]
    pivots = factors.shape[2]
    buffers = [rows0, rows1]
    solved = fetch_fronts(core, own, peer, 1, 0, pivots, buffers, sems.at[0])
    others = fetch_fronts(core, own, peer, 1, pivots, pivots, buffers, sems.at[1])
    mine = pl.ds(pl.multiple_of(core * half, half), half)
    theirs = pl.ds(pl.multiple_of((1 - core) * half, half), half)
    stores = [
        pltpu.make_async_copy(factors.at[k, mine, :], held.at[k, 0], sems.at[2, k])
        for k in range(2)
    ]
    stores.append(pltpu.make_async_copy(factors.at[core, theirs, :], given.at[0], sems.at[2, 2]))
    for store in stores:
        store.start()
    pivot_sum[...] = jnp.zeros(pivot_sum.shape, f32)
    low_sum[...] = jnp.zeros(low_sum.shape, f32)
    place_row = 2 * chip + core
    for j in range(4):
        part = slice(j * TILE, (j + 1) * TILE)
        rest = slice((4 + j) * TILE, (5 + j) * TILE)

        @pl.when(j <= place_row)
        def _(j=j, part=part):
            pivot_sum[((place_row * (place_row + 1)) >> 1) + j] = front[0, :, part]

        low_sum[chip, 4 * core + j] = front[1, :, part]
        low_sum[core, 8 + 4 * chip + j] = front[1, :, rest]
    for k in range(2):
        rows = buffers[k]
        wait_all(solved[k])
        solve_rows(rows, factors.at[k], inverses.at[k])
        store = pltpu.make_async_copy(
            rows.at[mine, pl.ds(0, pivots)], held.at[k, 1], sems.at[3, k]
        )
        store.start()
        stores.append(store)
        store = pltpu.make_async_copy(
            rows.at[theirs, pl.ds(0, pivots)], given.at[1], sems.at[3, 2]
        )
        pl.when(core == k)(store.start)
        if k:
            stores.append(store)
        left[k] = split_left(rows[:, :pivots])
        right[k] = split_right(rows[:, :pivots])

    def contribute(k, slot, pairs):
        rows = buffers[k]
        for a, b in pairs:
            first = slice(a * TILE, (a + 1) * TILE)
            second = slice(b * TILE, (b + 1) * TILE)
            there = slice((4 + b) * TILE, (5 + b) * TILE)
            block = rows[first, there] - parts_product(left[k, first], right[k, second])
            ra, rb = maps[slot, a], maps[slot, b]

            @pl.when(ra < 4)
            def _():
                spot = ((ra * (ra + 1)) >> 1) + rb
                pivot_sum[spot] = pivot_sum[spot] + block

            @pl.when(jnp.logical_and(ra >= 4, rb < 4))
            def _():
                spot = (ra - 4) >> 1, (ra & 1) * 4 + rb
                low_sum[spot] = low_sum[spot] + block

            @pl.when(rb >= 4)
            def _():
                spot = ra & 1, 8 + ((ra - 4) >> 1) * 4 + rb - 4
                low_sum[spot] = low_sum[spot] + block
                if a != b:
                    spot = rb & 1, 8 + ((rb - 4) >> 1) * 4 + ra - 4
                    low_sum[spot] = low_sum[spot] + block.T

    for k in range(2):
        slot = core + k
        wait_all(others[k])
        pl.when(core == 0 if k == 0 else live[0] > slot)(
            lambda k=k, slot=slot: contribute(k, slot, PAIRS[:HALF])
        )
        pl.when(live[0] > slot if k == 0 else jnp.logical_and(core == 1, live[0] > slot))(
            lambda k=k, slot=slot: contribute(k, slot, PAIRS[HALF:])
        )
    keep_pivot[...] = pivot_sum[pl.ds(core * HALF, HALF)]
    give_pivot[...] = pivot_sum[pl.ds((1 - core) * HALF, HALF)]
    keep_low[...] = low_sum[core]
    give_low[...] = low_sum[1 - core]
    wait_all(stores)


def parent_pivot_kernel(
    place, live, own, other, held, taken, factor, inverses, children, grid, stage, blank, sems
):
    core = place[0]
    loads = [pltpu.make_async_copy(held.at[k], stage.at[k], sems.at[k]) for k in range(2)]
    loads.append(pltpu.make_async_copy(taken, stage.at[2], sems.at[2]))
    for copy in loads:
        copy.start()
    blank[...] = jnp.zeros(blank.shape, f32)
    for side in range(2):

        @pl.when(core == side)
        def _(side=side):
            for n, (a, b) in enumerate(PAIRS):
                source = own if n // HALF == side else other
                grid[a * GRID + b] = source[n % HALF]

    spots = [
        jnp.where(core == 0, 0, 2),
        jnp.where(core == 0, 1, 0),
        jnp.where(core == 0, 2, 1),
    ]
    stores = [
        pltpu.make_async_copy(stage.at[spots[slot]], children.at[slot], sems.at[slot])
        for slot in range(3)
    ]

    def pass_children():
        wait_all(loads)
        for slot, store in enumerate(stores):
            clear = pltpu.make_async_copy(blank, children.at[slot], sems.at[slot])
            pl.when(live[0] > slot)(store.start)
            pl.when(live[0] <= slot)(clear.start)

    factor_pivots([grid], [inverses], pass_children)
    grid_to_matrix(grid, factor)
    wait_all(stores)


def parent_lower_kernel(place, factor, inverses, own, other, corner, panels, update, rows):
    core, chip = place[0], place[1]
    for side in range(2):

        @pl.when(core == side)
        def _(side=side):
            for n in range(16):
                source = own if n // 8 == side else other
                rows[n // 4 * TILE : (n // 4 + 1) * TILE, n % 4 * TILE : (n % 4 + 1) * TILE] = (
                    source[n % 8]
                )

    solve_rows(rows, factor, inverses)
    mine = pl.ds(pl.multiple_of((2 * chip + core) * TILE, TILE), TILE)
    panels[0] = factor[mine, :]
    panels[1] = rows[mine, :]
    left = split_left(rows[mine, :])
    for j in range(4):
        part = slice(j * TILE, (j + 1) * TILE)
        update[:, part] = corner[j] - parts_product(left, split_right(rows[part, :]))


SMEM = pl.BlockSpec(memory_space=pltpu.SMEM)
VMEM = pl.BlockSpec(memory_space=pltpu.VMEM)
ANY = pl.BlockSpec(memory_space=pl.ANY)


def run(kernel, name, flops, shapes, specs, scratch, *operands, out_specs=None):
    return pl.pallas_call(
        kernel,
        out_shape=[jax.ShapeDtypeStruct(s, f32) for s in shapes],
        in_specs=specs,
        out_specs=out_specs or [VMEM] * len(shapes),
        scratch_shapes=scratch,
        name=name,
        cost_estimate=pl.CostEstimate(flops=flops, bytes_accessed=1 << 22, transcendentals=0),
        compiler_params=pltpu.CompilerParams(vmem_limit_bytes=48 << 20),
    )(*operands)


def on_device(child_fronts, child_live, row_map, parent_fronts):
    quarter = child_fronts.shape[2]
    pivots = 2 * quarter
    core = lax.axis_index("front")
    chip = lax.axis_index("leaf") % 2
    leaves = lax.axis_size("leaf")
    blocks = (TILE, TILE)

    def swap_core(value):
        return lax.ppermute(value, "front", [(0, 1), (1, 0)])

    def swap_chip(value):
        return lax.ppermute(value, "leaf", [(i, i ^ 1) for i in range(leaves)])

    place = jnp.stack([core, chip]).astype(jnp.int32)
    top = lax.dynamic_slice(child_fronts, (1 - core, 0, 0, 0), (2, 1, quarter, pivots))[:, 0]
    peer_top = swap_core(top)
    low = lax.dynamic_slice(child_fronts, (1 - core, 1, 0, 0), (2, 1, quarter, 2 * pivots))[:, 0]
    peer_low = swap_core(low)
    factors, inverses = run(
        pivot_kernel,
        "pivot",
        10**10,
        [(2, pivots, pivots), (2, 4, *blocks)],
        [SMEM, ANY, ANY],
        [pltpu.VMEM((GRID * GRID, *blocks), f32)] * 2 + [pltpu.SemaphoreType.DMA((4,))],
        place,
        child_fronts,
        peer_top,
    )
    held, given, keep_pivot, give_pivot, keep_low, give_low = run(
        lower_kernel,
        "lower",
        4 * 10**9,
        [
            (2, 2, quarter, pivots),
            (2, quarter, pivots),
            (HALF, *blocks),
            (HALF, *blocks),
            (16, *blocks),
            (16, *blocks),
        ],
        [SMEM, SMEM, SMEM, ANY, ANY, VMEM, VMEM, VMEM],
        [
            pltpu.VMEM((pivots, 2 * pivots), f32),
            pltpu.VMEM((pivots, 2 * pivots), f32),
            pltpu.VMEM((2, pivots, 3 * pivots), jnp.bfloat16),
            pltpu.VMEM((2, pivots, 3 * pivots), jnp.bfloat16),
            pltpu.VMEM((2 * HALF, *blocks), f32),
            pltpu.VMEM((2, 16, *blocks), f32),
            pltpu.SemaphoreType.DMA((4, 4)),
        ],
        place,
        child_live,
        row_map,
        child_fronts,
        peer_low,
        factors,
        inverses,
        parent_fronts[0],
        out_specs=[ANY, ANY] + [VMEM] * 4,
    )
    chip_pivot = keep_pivot + swap_core(give_pivot)
    give_low, given, far_pivot = lax.optimization_barrier((give_low, given, chip_pivot))
    taken = swap_core(given)
    half_pivot = chip_pivot + swap_chip(far_pivot)
    chip_low = keep_low + swap_core(give_low)
    chip_rows = chip_low[8:].reshape(2, 4, *blocks)
    own_rows = lax.dynamic_index_in_dim(chip_rows, chip, 0, keepdims=False)
    far_rows = lax.dynamic_index_in_dim(chip_rows, 1 - chip, 0, keepdims=False)
    half_pivot, far_low, far_rows = lax.optimization_barrier(
        (half_pivot, chip_low[:8], far_rows)
    )
    other_pivot = swap_core(half_pivot)
    arrived_low = swap_chip(far_low)
    arrived_rows = swap_chip(far_rows)
    factor, parent_inverses, child_panels = run(
        parent_pivot_kernel,
        "parent_pivot",
        10**10,
        [(pivots, pivots), (4, *blocks), child_fronts.shape[:3] + (pivots,)],
        [SMEM, SMEM, VMEM, VMEM, ANY, ANY],
        [
            pltpu.VMEM((GRID * GRID, *blocks), f32),
            pltpu.VMEM((3, 2, quarter, pivots), f32),
            pltpu.VMEM((2, quarter, pivots), f32),
            pltpu.SemaphoreType.DMA((3,)),
        ],
        place,
        child_live,
        half_pivot,
        other_pivot,
        held,
        taken,
        out_specs=[VMEM, VMEM, ANY],
    )
    factor, arrived_low, arrived_rows = lax.optimization_barrier(
        (factor, arrived_low, arrived_rows)
    )
    half_low = chip_low[:8] + arrived_low
    corner = own_rows + arrived_rows
    other_low = swap_core(half_low)
    panels, update = run(
        parent_lower_kernel,
        "parent_lower",
        10**9,
        [(2, TILE, pivots), (TILE, pivots)],
        [SMEM] + [VMEM] * 5,
        [pltpu.VMEM((pivots, pivots), f32)],
        place,
        factor,
        parent_inverses,
        half_low,
        other_low,
        corner,
    )
    return (child_panels, panels[None], update[None])


def solution(mesh):
    placed = (
        P("leaf", None, "front", None),
        P("leaf"),
        P("leaf", None),
        P("leaf", None, "front", None),
    )
    return jax.shard_map(
        on_device,
        mesh=mesh,
        in_specs=placed,
        out_specs=(
            P("leaf", None, "front", None),
            P("leaf", None, "front", None),
            P("leaf", "front", None),
        ),
        check_vma=False,
    )
```
